256 devices in a mesh: st: 32 (over z, y), tm: 4 (over x_lo, core), pol: 2 (over x_hi).
Axes of the slice: x: 4 (x_hi: 2, x_lo: 2; x = x_hi * 2 + x_lo), y: 4, z: 8, core: 2. Of those that a mesh axis runs over, the one named last changes fastest.
Arguments:
- samples: bfloat16 [512, 262144], P('st', 'tm'), may hold values from -6 to 6
- history: bfloat16 [512, 24576], P('st'), may hold values from -6 to 6
- station_order: int32 [256], replicated, may hold values from 0 to 255, each once
- channel_order: int32 [2048], replicated, may hold values from 0 to 2047, each once
- flagged: int32 [256], replicated, may hold values 0 or 1
Outputs:
- packed: float32 [2048, 512, 512], P(('st', 'tm', 'pol'))
The draws below stay inside these ranges and needn't reach their ends.
Inputs may be any that keep to these rules, and one draw needn't show every extreme that they name: `station_order`: each station number appears once. `channel_order`: each channel appears once.
All inputs are finite; a program needn't handle non-finite values.
Results may differ from the reference program's by a relative error of at most 0.0082.
Values may be sent and summed in bfloat16 or wider, within the bound.
A program may use at most 256 MiB of HBM per device.

```python
import math
import jax
import jax.numpy as jnp
from jax import lax

STATIONS = 256
NFFT = 8192
FRAME_A = 32
CH = 2048
TAPS = 4
INPUTS = 512
SAMPLES = 262144


def plant(array, key, least, top_value):
    place = [jax.random.randint(jax.random.fold_in(key, axis), (), 0, length) for axis, length in enumerate(array.shape)]
    main_axis = array.shape.index(max(array.shape))
    neighbour = place[:main_axis] + [(place[main_axis] + 1) % array.shape[main_axis]] + place[main_axis + 1:]
    return array.at[tuple(place)].set(least).at[tuple(neighbour)].set(top_value)


def levels(key, extent, shards, smallest, largest):
    def one(dim, shards_of):
        draws = jax.random.uniform(jax.random.fold_in(jax.random.fold_in(key, 6), dim), (shards_of,), jnp.float32, smallest / len(shards), largest / len(shards))
        return jnp.repeat(jnp.exp(draws), extent[dim] // shards_of).reshape((-1,) + (1,) * (len(extent) - dim - 1))

    level = one(*shards[0])
    for cut in shards[1:]:
        level = level * one(*cut)
    return level


def scatter_about(own_key, dims, deviation, most, pieces=(), dtype=jnp.bfloat16):
    entries = jax.random.normal(own_key, dims, jnp.float32) * deviation
    if len(pieces) > 0:
        entries = levels(own_key, dims, pieces, -0.22, 0.18) * entries
    return jnp.clip(entries, min=-most, max=most).astype(dtype)


def setup_inputs(seed: int = 0) -> dict:
    splits = jax.random.split(jax.random.key(seed), 6)
    samples = scatter_about(splits[0], (INPUTS, SAMPLES), 1.0, 6.0, ((0, 32), (1, 4)))
    history = scatter_about(splits[1], (INPUTS, (TAPS - 1) * NFFT), 1.0, 6.0, ((0, 32),))
    station_order = jax.random.permutation(splits[2], STATIONS).astype(jnp.int32)
    channel_order = jax.random.permutation(splits[3], CH).astype(jnp.int32)
    flagged = plant((jax.random.randint(splits[4], (STATIONS,), 0, 8) < 1).astype(jnp.int32), jax.random.fold_in(splits[4], 1), 0, 1)
    return dict(samples=samples, history=history, station_order=station_order, channel_order=channel_order, flagged=flagged)


def filter_window(tap_count, frame_size):
    length = tap_count * frame_size
    offsets = jnp.arange(length).astype(jnp.float32) + 0.5
    centred = (offsets - 0.5 * length) / frame_size
    tapering = 0.5 - 0.5 * jnp.cos(offsets * (2.0 * math.pi / length))
    return (jnp.sinc(centred) * tapering).reshape(tap_count, frame_size)

def polyphase(row_block, weights, spec_count):
    row_total = row_block.shape[0]
    tap_count, frame_size = weights.shape
    running = jnp.zeros((row_total, spec_count, frame_size), jnp.float32)
    for tap_index in range(tap_count):
        section = row_block[:, tap_index * frame_size:(tap_index + spec_count) * frame_size]
        section = section.reshape(row_total, spec_count, frame_size)
        running = running + section.astype(jnp.float32) * weights[tap_index]
    return running.astype(jnp.bfloat16).reshape(row_total * spec_count, frame_size)

def trig_pair(left, right, modulus, amplitude):
    turn_count = left.astype(jnp.int32)[:, None] * right.astype(jnp.int32)[None, :] % modulus
    angles = turn_count.astype(jnp.float32) * (2.0 * math.pi / modulus)
    cosine = (jnp.cos(angles) * amplitude).astype(jnp.bfloat16)
    sine_part = (-(jnp.sin(angles) * amplitude)).astype(jnp.bfloat16)
    return (cosine, sine_part)

def product_high(form, left, right):
    return jnp.einsum(form, left.astype(jnp.float32), right.astype(jnp.float32), precision=lax.Precision.HIGHEST)

def frame_transform(filtered, channels, first_len):
    row_total, frame_size = filtered.shape
    second_len = frame_size // first_len
    half_len = second_len // 2
    first_idx = jnp.arange(first_len).astype(jnp.int32)
    second_idx = jnp.arange(second_len).astype(jnp.int32)
    half_idx = jnp.arange(half_len).astype(jnp.int32)
    first_cos, first_sin = trig_pair(first_idx, first_idx, first_len, 1.0 / math.sqrt(first_len))
    blocks = filtered.reshape(row_total, first_len, second_len)
    segment_re = product_high('rab,ae->reb', blocks, first_cos)
    segment_im = product_high('rab,ae->reb', blocks, first_sin)
    twist_turns = first_idx[:, None] * second_idx[None, :] % frame_size
    twist_angles = twist_turns.astype(jnp.float32) * (2.0 * math.pi / frame_size)
    twist_cos = jnp.cos(twist_angles)
    twist_sin = jnp.sin(twist_angles)
    twist_re = (segment_re * twist_cos + segment_im * twist_sin).astype(jnp.bfloat16)
    twist_im = (segment_im * twist_cos - segment_re * twist_sin).astype(jnp.bfloat16)
    second_cos, second_sin = trig_pair(second_idx, half_idx, second_len, 1.0 / math.sqrt(second_len))
    full_re = product_high('reb,bf->ref', twist_re, second_cos) - product_high('reb,bf->ref', twist_im, second_sin)
    full_im = product_high('reb,bf->ref', twist_re, second_sin) + product_high('reb,bf->ref', twist_im, second_cos)
    channels = channels.astype(jnp.int32)
    column = (channels % first_len * half_len + channels // first_len).astype(jnp.int32)
    flat_re = full_re.reshape(row_total, first_len * half_len)[:, column]
    flat_im = full_im.reshape(row_total, first_len * half_len)[:, column]
    return jnp.stack([flat_re, flat_im], axis=1)

def input_rows(station_order):
    station_total = station_order.shape[0]
    inverse = jnp.zeros((station_total,), jnp.int32).at[station_order.astype(jnp.int32)].set(jnp.arange(station_total).astype(jnp.int32))
    polarity = jnp.tile(jnp.arange(2).astype(jnp.int32), station_total)
    return (2 * jnp.repeat(inverse, 2) + polarity).astype(jnp.int32)

def packed_visibility(values, norm_scale):
    input_count, spec_count, pair_count, slot_count = values.shape
    arranged = values.transpose(3, 0, 1, 2)
    stacked = arranged.reshape(slot_count, input_count, spec_count * 2)
    swapped = jnp.stack([-arranged[..., 1], arranged[..., 0]], axis=-1).reshape(slot_count, input_count, spec_count * 2)
    combined = jnp.concatenate([stacked, swapped], axis=1)
    visible = jnp.einsum('sik,sjk->sij', stacked, combined, precision=lax.Precision.HIGHEST)
    indices = jnp.arange(input_count)
    upper_half = indices[:, None] <= indices[None, :]
    return jnp.where(upper_half[None], visible[:, :, :input_count], visible[:, :, input_count:]) * norm_scale

def reference(samples, history, station_order, channel_order, flagged):
    spec_total = samples.shape[1] // NFFT
    weights = filter_window(TAPS, NFFT)
    stream = jnp.concatenate([history, samples], axis=1)
    block_rows = min(16, INPUTS)
    block_count = INPUTS // block_rows
    keeping = (1 - flagged[station_order.astype(jnp.int32)]).astype(jnp.float32)
    keep_rows = jnp.repeat(keeping, 2)
    stream_blocks = stream.reshape(block_count, block_rows, stream.shape[1])
    keep_blocks = keep_rows.reshape(block_count, block_rows)

    def transform(operand):
        row_block, keep_block = operand
        filtered = polyphase(row_block, weights, spec_total)
        product = frame_transform(filtered, channel_order, FRAME_A)
        product = product.reshape(block_rows, spec_total, 2, CH) * keep_block[:, None, None, None]
        return product.astype(jnp.bfloat16)
    spectra = lax.map(transform, (stream_blocks, keep_blocks)).reshape(INPUTS, spec_total, 2, CH)
    ordered = spectra[input_rows(station_order)]
    slot_block = min(16, CH)
    slot_groups = CH // slot_block
    grouped = ordered.reshape(INPUTS, spec_total, 2, slot_groups, slot_block).transpose(3, 0, 1, 2, 4)
    norm_scale = 1.0 / spec_total

    def correlate(group):
        return packed_visibility(group.astype(jnp.float32), norm_scale)
    return lax.map(correlate, grouped).reshape(CH, INPUTS, INPUTS)
```

```python
import functools
import math

import jax
import jax.numpy as jnp
import numpy as np
from jax import lax
from jax.experimental import pallas as pl
from jax.experimental.pallas import tpu as pltpu
from jax.sharding import PartitionSpec as P

import ml_dtypes

NFFT = 8192
FRAME_A = 32
FRAME_B = NFFT // FRAME_A
CH = 2048
TAPS = 4
LEAD = TAPS - 1
ROWS = 8
FRAMES = 8
PEERS = 256
MESH = pl.DeviceIdType.MESH
Z_OFFSETS = (1, 7, 2, 6, 3, 5, 4, 0)
BF16 = jnp.bfloat16
F32 = jnp.float32


def constants():
    bf = ml_dtypes.bfloat16
    length = TAPS * NFFT
    m = np.arange(length) + 0.5
    window = np.sinc((m - 0.5 * length) / NFFT) * (0.5 - 0.5 * np.cos(m * (2.0 * math.pi / length)))
    window = window.reshape(TAPS, NFFT).astype(np.float32)
    a = np.arange(FRAME_A)
    angle = (a[:, None] * a[None, :] % FRAME_A) * (2.0 * math.pi / FRAME_A)
    cos = np.cos(angle) / math.sqrt(FRAME_A)
    sin = -np.sin(angle) / math.sqrt(FRAME_A)
    first = np.concatenate([cos[:, :17], sin[:, 1:16]], axis=1).T.astype(bf)
    first = np.kron(first.astype(np.float32), np.eye(ROWS, dtype=np.float32)).astype(bf)
    b = np.arange(FRAME_B)
    twist = (a[:, None] * b[None, :] % NFFT) * (2.0 * math.pi / NFFT)
    twist_cos = np.repeat(np.cos(twist), ROWS, axis=0).astype(np.float32)
    twist_sin = np.repeat(np.sin(twist), ROWS, axis=0).astype(np.float32)
    f = np.arange(CH // FRAME_A)
    angle = (b[:, None] * f[None, :] % FRAME_B) * (2.0 * math.pi / FRAME_B)
    cos = (np.cos(angle) / math.sqrt(FRAME_B)).astype(bf)
    sin = (-np.sin(angle) / math.sqrt(FRAME_B)).astype(bf)
    second = np.concatenate([np.concatenate([cos, sin], 1), np.concatenate([-sin, cos], 1)], 0)
    t, p, f = np.meshgrid(np.arange(FRAMES), np.arange(2), np.arange(64), indexing="ij")
    perm = np.zeros((1024, 1024), np.float32)
    perm[(t * 128 + p * 64 + f).ravel(), (f * 16 + p * 8 + t).ravel()] = 1
    return window, first, twist_cos, twist_sin, second, perm.astype(bf)


def filterbank_kernel(
    place, samples, halo, window_h, first_h, tcos_h, tsin_h, second_h, perm_h, keep, out,
    stream, window, first, tcos, tsin, second, perm, filtered, lanes, full, sem,
):
    rows = pl.ds(pl.multiple_of(lax.axis_index("pol") * ROWS, ROWS), ROWS)
    lead = LEAD * NFFT
    moves = [
        (samples.at[rows], stream.at[:, pl.ds(lead, FRAMES * NFFT)]),
        (halo, stream.at[:, pl.ds(0, lead)]),
        (window_h, window), (first_h, first), (tcos_h, tcos), (tsin_h, tsin),
        (second_h, second), (perm_h, perm),
    ]
    copies = [pltpu.make_async_copy(s, d, sem.at[i]) for i, (s, d) in enumerate(moves)]
    for c in copies:
        c.start()
    for c in copies[:3]:
        c.wait()

    def taps(i, carry):
        parts = []
        for half in range(2):
            off = i // 2 * 512 + half * 256 + i % 2 * 128
            w = [
                jnp.broadcast_to(window[k : k + 1, pl.ds(pl.multiple_of(off, 128), 128)], (ROWS, 128))
                for k in range(TAPS)
            ]
            x = [
                stream[:, pl.ds(pl.multiple_of(off + j * NFFT, 128), 128)].astype(F32)
                for j in range(FRAMES + LEAD)
            ]
            parts.append([sum(w[k] * x[t + k] for k in range(TAPS)) for t in range(FRAMES)])
        for t in range(FRAMES):
            block = jnp.concatenate([parts[0][t], parts[1][t]], axis=0).astype(BF16)
            filtered[t, pl.ds(pl.multiple_of(i // 2 * 16, 16), 16), pl.ds(pl.multiple_of(i % 2 * 128, 128), 128)] = block
        return carry

    lax.fori_loop(0, 32, taps, 0)
    for c in copies[3:7]:
        c.wait()

    def frame(t, carry):
        seg = jnp.dot(first[...], filtered[t], preferred_element_type=F32)
        res, ims = [], []
        for e in range(FRAME_A):
            s = min(e, FRAME_A - e)
            rs = slice(e * ROWS, (e + 1) * ROWS)
            c, n = tcos[rs, :], tsin[rs, :]
            re = seg[s * ROWS : (s + 1) * ROWS]
            if s in (0, 16):
                res.append(re * c)
                ims.append(-(re * n))
            else:
                im = seg[(16 + s) * ROWS : (17 + s) * ROWS]
                if e < 16:
                    res.append(re * c + im * n)
                    ims.append(im * c - re * n)
                else:
                    res.append(re * c - im * n)
                    ims.append(-(im * c) - re * n)
        tw = jnp.concatenate(
            [jnp.concatenate(res, axis=0).astype(BF16), jnp.concatenate(ims, axis=0).astype(BF16)], axis=1
        )
        spec = jnp.dot(tw, second[...], preferred_element_type=F32) * keep[...]
        lanes[:, pl.ds(pl.multiple_of(t * 128, 128), 128)] = spec.astype(BF16)
        return carry

    lax.fori_loop(0, FRAMES, frame, 0)
    copies[7].wait()
    for q in range(4):
        turned = jnp.dot(lanes[...], perm[:, q * 256 : (q + 1) * 256], preferred_element_type=F32)
        for h in range(2):
            block = 2 * q + h
            full[block * 32 : (block + 1) * 32] = turned[:, h * 128 : (h + 1) * 128].reshape(32, ROWS, 128)

    lane = lax.broadcasted_iota(jnp.int32, (ROWS, 128), 1) // 16

    def gather(d, carry):
        acc = None
        for j in range(8):
            g = d * 8 + j
            v = pltpu.roll(full[place[0, g]], place[1, g], 1)
            acc = v if acc is None else jnp.where(lane == j, v, acc)
        out[d] = acc.astype(BF16)
        return carry

    lax.fori_loop(0, PEERS, gather, 0, unroll=2)


def filterbank(place, samples, halo, keep):
    consts = [jnp.asarray(c) for c in constants()]
    anyspec = pl.BlockSpec(memory_space=pl.ANY)
    vmem = pl.BlockSpec(memory_space=pltpu.VMEM)
    return pl.pallas_call(
        filterbank_kernel,
        out_shape=jax.ShapeDtypeStruct((PEERS, 8, 128), BF16),
        in_specs=[pl.BlockSpec(memory_space=pltpu.SMEM)] + [anyspec] * 8 + [vmem],
        out_specs=vmem,
        scratch_shapes=[
            pltpu.VMEM((ROWS, (FRAMES + LEAD) * NFFT), BF16),
            pltpu.VMEM((TAPS, NFFT), F32),
            pltpu.VMEM((256, 256), BF16),
            pltpu.VMEM((256, 256), F32),
            pltpu.VMEM((256, 256), F32),
            pltpu.VMEM((512, 128), BF16),
            pltpu.VMEM((1024, 1024), BF16),
            pltpu.VMEM((FRAMES, 256, 256), BF16),
            pltpu.VMEM((256, 1024), BF16),
            pltpu.VMEM((256, ROWS, 128), F32),
            pltpu.SemaphoreType.DMA((8,)),
        ],
        compiler_params=pltpu.CompilerParams(vmem_limit_bytes=40 << 20),
        name="filterbank",
    )(place, samples, halo, *consts, keep)


def exchange_kernel(src, dst, send_sem, recv_sem, own_sem):
    st, tm, pol = lax.axis_index("st"), lax.axis_index("tm"), lax.axis_index("pol")
    z, y, w = st // 4, st % 4, tm * 2 + pol
    zs = [(z + o) % 8 for o in Z_OFFSETS]

    def each(action):
        def step(o, carry):
            yy, ww = (y + o % 4) % 4, (w + o // 4) % 8
            for j in range(8):
                s = zs[j] * 4 + yy
                if Z_OFFSETS[j]:
                    action(s, ww // 2, ww % 2)
                else:
                    pl.when(o != 0)(lambda s=s: action(s, ww // 2, ww % 2))
            return carry

        lax.fori_loop(0, 32, step, 0)

    barrier = pltpu.get_barrier_semaphore()
    each(lambda a, b, c: pl.semaphore_signal(barrier, inc=1, device_id=(a, b, c), device_id_type=MESH))
    pl.semaphore_wait(barrier, PEERS - 1)
    slot = st * 2 + pol

    def send(a, b, c):
        pltpu.make_async_remote_copy(
            src.at[a * 8 + b * 2 + c], dst.at[tm * 64 + slot], send_sem, recv_sem,
            device_id=(a, b, c), device_id_type=MESH,
        ).start()

    each(send)
    own = pltpu.make_async_copy(src.at[st * 8 + w], dst.at[tm * 64 + slot], own_sem)
    own.start()
    own.wait()
    part = pl.ds(0, PEERS - 1)
    pltpu.make_async_copy(src.at[part], dst.at[part], send_sem).wait()
    pltpu.make_async_copy(src.at[part], dst.at[part], recv_sem).wait()


def exchange(messages):
    vmem = pl.BlockSpec(memory_space=pltpu.VMEM)
    return pl.pallas_call(
        exchange_kernel,
        out_shape=jax.ShapeDtypeStruct((PEERS, 8, 128), BF16),
        in_specs=[vmem],
        out_specs=vmem,
        scratch_shapes=[pltpu.SemaphoreType.DMA] * 3,
        compiler_params=pltpu.CompilerParams(collective_id=0, has_side_effects=True),
        name="exchange",
    )(messages)


def correlate_kernel(turned, target, out, parts, swapped):
    slot = pl.program_id(0)

    @pl.when(slot == 0)
    def _():
        inputs = lax.broadcasted_iota(jnp.int32, (512, 512), 1)
        onehot = (target[...] == inputs).astype(F32).astype(BF16)
        for tm in range(4):
            got = lax.dot_general(
                turned[tm], onehot, (((0,), (0,)), ((), ())), preferred_element_type=F32
            )
            for s in range(8):
                re, im = got[16 * s : 16 * s + 8], got[16 * s + 8 : 16 * s + 16]
                parts[s, 16 * tm : 16 * tm + 16] = jnp.concatenate([re, im], axis=0).astype(BF16)
                swapped[s, 16 * tm : 16 * tm + 16] = jnp.concatenate([-im, re], axis=0).astype(BF16)

    part, swap = parts[slot], swapped[slot]

    def product(i, right, j):
        return lax.dot_general(
            part[:, i * 256 : i * 256 + 256], right[:, j * 256 : j * 256 + 256],
            (((0,), (0,)), ((), ())), preferred_element_type=F32,
        )

    upper = lax.broadcasted_iota(jnp.int32, (256, 256), 0) <= lax.broadcasted_iota(jnp.int32, (256, 256), 1)
    for i in range(2):
        for j in range(2):
            if i == j:
                block = jnp.where(upper, product(i, part, j), product(i, swap, j))
            else:
                block = product(i, part if i < j else swap, j)
            out[0, i * 256 : i * 256 + 256, j * 256 : j * 256 + 256] = block * (1.0 / 32)


def correlate(turned, target):
    return pl.pallas_call(
        correlate_kernel,
        out_shape=jax.ShapeDtypeStruct((8, 512, 512), F32),
        grid=(8,),
        in_specs=[
            pl.BlockSpec((4, 512, 128), lambda s: (0, 0, 0)),
            pl.BlockSpec((512, 1), lambda s: (0, 0)),
        ],
        out_specs=pl.BlockSpec((1, 512, 512), lambda s: (s, 0, 0)),
        scratch_shapes=[pltpu.VMEM((8, 64, 512), BF16), pltpu.VMEM((8, 64, 512), BF16)],
        compiler_params=pltpu.CompilerParams(vmem_limit_bytes=24 << 20),
        name="correlate",
    )(turned, target)


def body(samples, history, station_order, channel_order, flagged):
    tm, pol = lax.axis_index("tm"), lax.axis_index("pol")
    length = samples.shape[1]
    lead = LEAD * NFFT
    first_row = pol * ROWS
    tail = lax.dynamic_slice(samples, (first_row, length - lead), (ROWS, lead))
    earlier = lax.ppermute(tail, "tm", [(i, i + 1) for i in range(3)])
    own = lax.dynamic_slice(history, (first_row, 0), (ROWS, lead))
    halo = jnp.where(tm == 0, own, earlier)
    f = channel_order // FRAME_A
    slots = jnp.arange(CH) % 8
    place = jnp.stack([f // 8 * 32 + channel_order % FRAME_A, (slots - f % 8) * 16 % 128])
    stations = lax.dynamic_slice_in_dim(station_order, lax.axis_index("st") * 8 + pol * 4, 4)
    keep = jnp.repeat(1 - flagged[stations], 2).astype(F32)
    keep = jnp.tile(keep[None], (FRAME_A, 1)).reshape(FRAME_A * ROWS, 1)
    messages = filterbank(place, samples, halo, keep)
    turned = exchange(messages).reshape(4, 512, 128)
    target = (2 * station_order[:, None] + jnp.arange(2)[None]).reshape(512, 1)
    return correlate(turned, target)


def solution(mesh):
    return jax.shard_map(
        body,
        mesh=mesh,
        in_specs=(P("st", "tm"), P("st", None), P(), P(), P()),
        out_specs=P(("st", "tm", "pol"), None, None),
        check_vma=False,
    )
```

```python
import functools
import math

import jax
import jax.numpy as jnp
import numpy as np
from jax import lax
from jax.experimental import pallas as pl
from jax.experimental.pallas import tpu as pltpu
from jax.sharding import PartitionSpec as P

import ml_dtypes

NFFT = 8192
FRAME_A = 32
FRAME_B = NFFT // FRAME_A
CH = 2048
TAPS = 4
LEAD = TAPS - 1
ROWS = 8
FRAMES = 8
PEERS = 256
MESH = pl.DeviceIdType.MESH
Z_OFFSETS = (1, 7, 2, 6, 3, 5, 4, 0)
BF16 = jnp.bfloat16
F32 = jnp.float32


def constants():
    bf = ml_dtypes.bfloat16
    length = TAPS * NFFT
    m = np.arange(length) + 0.5
    window = np.sinc((m - 0.5 * length) / NFFT) * (0.5 - 0.5 * np.cos(m * (2.0 * math.pi / length)))
    window = window.reshape(TAPS, NFFT).astype(np.float32)
    a = np.arange(FRAME_A)
    angle = (a[:, None] * a[None, :] % FRAME_A) * (2.0 * math.pi / FRAME_A)
    cos = np.cos(angle) / math.sqrt(FRAME_A)
    sin = -np.sin(angle) / math.sqrt(FRAME_A)
    first = np.concatenate([cos[:, :17], sin[:, 1:16]], axis=1).T.astype(bf)
    first = np.kron(first.astype(np.float32), np.eye(ROWS, dtype=np.float32)).astype(bf)
    b = np.arange(FRAME_B)
    twist = (a[:, None] * b[None, :] % NFFT) * (2.0 * math.pi / NFFT)
    twist_cos = np.repeat(np.cos(twist), ROWS, axis=0).astype(np.float32)
    twist_sin = np.repeat(np.sin(twist), ROWS, axis=0).astype(np.float32)
    f = np.arange(CH // FRAME_A)
    angle = (b[:, None] * f[None, :] % FRAME_B) * (2.0 * math.pi / FRAME_B)
    cos = (np.cos(angle) / math.sqrt(FRAME_B)).astype(bf)
    sin = (-np.sin(angle) / math.sqrt(FRAME_B)).astype(bf)
    second = np.concatenate([np.concatenate([cos, sin], 1), np.concatenate([-sin, cos], 1)], 0)
    t, p, f = np.meshgrid(np.arange(FRAMES), np.arange(2), np.arange(64), indexing="ij")
    perm = np.zeros((1024, 1024), np.float32)
    perm[(t * 128 + p * 64 + f).ravel(), (f * 16 + p * 8 + t).ravel()] = 1
    return window, first, twist_cos, twist_sin, second, perm.astype(bf)


def spectra_kernel(
    channels, stations, flags, samples, history, window_h, first_h, tcos_h, tsin_h, second_h, perm_h, out, onehot,
    stream, window, first, tcos, tsin, second, perm, filtered, lanes, full, messages,
    sem, lead_sem, lead_send, send_sem, recv_sem, own_sem,
):
    st, tm, pol = lax.axis_index("st"), lax.axis_index("tm"), lax.axis_index("pol")
    z, y, w = st // 4, st % 4, tm * 2 + pol
    zs = [(z + o) % 8 for o in Z_OFFSETS]

    def each(action, o):
        yy, ww = (y + o % 4) % 4, (w + o // 4) % 8
        for j in range(8):
            action(j, zs[j] * 4 + yy, ww // 2, ww % 2)

    def when_other(j, o, action):
        if Z_OFFSETS[j]:
            action()
        else:
            pl.when(o != 0)(action)

    lead = LEAD * NFFT
    half = lead // 2
    rows = pl.ds(pl.multiple_of(pol * ROWS, ROWS), ROWS)
    moves = [
        (samples.at[rows], stream.at[:, pl.ds(lead, FRAMES * NFFT)]),
        (window_h, window), (first_h, first), (tcos_h, tcos), (tsin_h, tsin),
        (second_h, second), (perm_h, perm),
    ]
    copies = [pltpu.make_async_copy(s, d, sem.at[i]) for i, (s, d) in enumerate(moves)]
    for c in copies:
        c.start()
    before = pltpu.make_async_copy(history.at[rows], stream.at[:, pl.ds(0, lead)], sem.at[7])
    pl.when(tm == 0)(before.start)

    barrier = pltpu.get_barrier_semaphore()

    def greet(o, carry):
        def signal(j, a, b, c):
            when_other(j, o, lambda: pl.semaphore_signal(
                barrier, inc=1, device_id=(a, b, c), device_id_type=MESH
            ))

        each(signal, o)
        return carry

    lax.fori_loop(0, 32, greet, 0)
    for c in copies[:2]:
        c.wait()

    def taps(lo, hi):
        def step(i, carry):
            parts = []
            for h in range(2):
                off = i // 2 * 512 + h * 256 + i % 2 * 128
                w = [
                    jnp.broadcast_to(window[k : k + 1, pl.ds(pl.multiple_of(off, 128), 128)], (ROWS, 128))
                    for k in range(TAPS)
                ]
                x = {
                    j: stream[:, pl.ds(pl.multiple_of(off + j * NFFT, 128), 128)].astype(F32)
                    for j in range(lo, hi + LEAD)
                }
                parts.append([sum(w[k] * x[t + k] for k in range(TAPS)) for t in range(lo, hi)])
            for t in range(lo, hi):
                block = jnp.concatenate([parts[0][t - lo], parts[1][t - lo]], axis=0).astype(BF16)
                filtered[
                    t, pl.ds(pl.multiple_of(i // 2 * 16, 16), 16), pl.ds(pl.multiple_of(i % 2 * 128, 128), 128)
                ] = block
            return carry

        lax.fori_loop(0, 32, step, 0)

    row = lax.broadcasted_iota(jnp.int32, (ROWS, 128), 0) // 2
    keep = jnp.zeros((ROWS, 128), F32)
    for i in range(ROWS // 2):
        flag = 1 - flags[stations[st * 8 + pol * 4 + i]]
        keep = jnp.where(row == i, flag.astype(F32), keep)
    keep = jnp.tile(keep, (FRAME_A, 1))

    def frame(t, carry):
        seg = jnp.dot(first[...], filtered[t], preferred_element_type=F32)
        res, ims = [], []
        for e in range(FRAME_A):
            s = min(e, FRAME_A - e)
            rs = slice(e * ROWS, (e + 1) * ROWS)
            c, n = tcos[rs, :], tsin[rs, :]
            re = seg[s * ROWS : (s + 1) * ROWS]
            if s in (0, 16):
                res.append(re * c)
                ims.append(-(re * n))
            else:
                im = seg[(16 + s) * ROWS : (17 + s) * ROWS]
                if e < 16:
                    res.append(re * c + im * n)
                    ims.append(im * c - re * n)
                else:
                    res.append(re * c - im * n)
                    ims.append(-(im * c) - re * n)
        tw = jnp.concatenate(
            [jnp.concatenate(res, axis=0).astype(BF16), jnp.concatenate(ims, axis=0).astype(BF16)], axis=1
        )
        spec = jnp.dot(tw, second[...], preferred_element_type=F32) * keep
        lanes[:, pl.ds(pl.multiple_of(t * 128, 128), 128)] = spec.astype(BF16)
        return carry

    taps(LEAD, FRAMES)
    for c in copies[2:6]:
        c.wait()
    lax.fori_loop(LEAD, FRAMES, frame, 0)

    pl.semaphore_wait(barrier, PEERS - 1)

    def lead_copy(i, b, c):
        src = samples.at[
            pl.ds(pl.multiple_of(c * ROWS, ROWS), ROWS), pl.ds(FRAMES * NFFT - lead + i * half, half)
        ]
        return pltpu.make_async_remote_copy(
            src, stream.at[:, pl.ds(i * half, half)], lead_send.at[i], lead_sem.at[i],
            device_id=(st, b, c), device_id_type=MESH,
        )

    after = (tm + 1) % 4
    across = (pol + after + 1) % 2
    leads = [lead_copy(0, after, pol), lead_copy(1, after, across)]

    @pl.when(tm != 3)
    def _():
        for c in leads:
            c.start()

    @pl.when(tm != 0)
    def _():
        for c in leads:
            c.wait_recv()

    pl.when(tm == 0)(before.wait)
    taps(0, LEAD)
    lax.fori_loop(0, LEAD, frame, 0)
    copies[6].wait()
    for q in range(4):
        turned = jnp.dot(lanes[...], perm[:, q * 256 : (q + 1) * 256], preferred_element_type=F32)
        for h in range(2):
            block = 2 * q + h
            full[block * 32 : (block + 1) * 32] = turned[:, h * 128 : (h + 1) * 128].reshape(32, ROWS, 128)

    lane = lax.broadcasted_iota(jnp.int32, (ROWS, 128), 1) // 16
    slot = tm * 64 + st * 2 + pol

    def send(o, carry):
        def one(j, a, b, c):
            peer = a * 8 + b * 2 + c
            acc = None
            for i in range(8):
                ch = channels[peer * 8 + i]
                v = full[ch // 256 * 32 + ch % 32]
                v = pltpu.roll(v, (8 + i - ch // 32 % 8) % 8 * 16, 1)
                acc = v if acc is None else jnp.where(lane == i, v, acc)
            messages[peer] = acc.astype(BF16)
            when_other(j, o, pltpu.make_async_remote_copy(
                messages.at[peer], out.at[slot], send_sem, recv_sem,
                device_id=(a, b, c), device_id_type=MESH,
            ).start)

        each(one, o)
        return carry

    lax.fori_loop(0, 32, send, 0)
    own = pltpu.make_async_copy(messages.at[st * 8 + w], out.at[slot], own_sem)
    own.start()

    inputs = lax.broadcasted_iota(jnp.int32, (16, 512), 1)
    pair = lax.broadcasted_iota(jnp.int32, (16, 512), 0)

    def target(i, carry):
        at = jnp.zeros((16, 512), jnp.int32)
        for p in range(8):
            at = jnp.where(pair // 2 == p, 2 * stations[i * 8 + p], at)
        onehot[pl.ds(pl.multiple_of(i * 16, 16), 16), :] = (at + pair % 2 == inputs).astype(F32).astype(BF16)
        return carry

    lax.fori_loop(0, 32, target, 0)

    @pl.when(tm != 3)
    def _():
        for c in leads:
            c.wait_send()

    own.wait()
    part = pl.ds(0, PEERS - 1)
    pltpu.make_async_copy(messages.at[part], out.at[part], send_sem).wait()
    pltpu.make_async_copy(messages.at[part], out.at[part], recv_sem).wait()


def spectra(channels, stations, flags, samples, history):
    consts = [jnp.asarray(c) for c in constants()]
    anyspec = pl.BlockSpec(memory_space=pl.ANY)
    vmem = pl.BlockSpec(memory_space=pltpu.VMEM)
    smem = pl.BlockSpec(memory_space=pltpu.SMEM)
    return pl.pallas_call(
        spectra_kernel,
        out_shape=[jax.ShapeDtypeStruct((PEERS, ROWS, 128), BF16), jax.ShapeDtypeStruct((512, 512), BF16)],
        in_specs=[smem] * 3 + [anyspec] * 8,
        out_specs=[vmem, vmem],
        scratch_shapes=[
            pltpu.VMEM((ROWS, (FRAMES + LEAD) * NFFT), BF16),
            pltpu.VMEM((TAPS, NFFT), F32),
            pltpu.VMEM((256, 256), BF16),
            pltpu.VMEM((256, 256), F32),
            pltpu.VMEM((256, 256), F32),
            pltpu.VMEM((512, 128), BF16),
            pltpu.VMEM((1024, 1024), BF16),
            pltpu.VMEM((FRAMES, 256, 256), BF16),
            pltpu.VMEM((256, 1024), BF16),
            pltpu.VMEM((256, ROWS, 128), F32),
            pltpu.VMEM((PEERS, ROWS, 128), BF16),
            pltpu.SemaphoreType.DMA((8,)),
            pltpu.SemaphoreType.DMA((2,)),
            pltpu.SemaphoreType.DMA((2,)),
        ] + [pltpu.SemaphoreType.DMA] * 3,
        compiler_params=pltpu.CompilerParams(
            vmem_limit_bytes=40 << 20, collective_id=0, has_side_effects=True
        ),
        name="spectra",
    )(channels, stations, flags, samples, history, *consts)


def correlate_kernel(turned, onehot, out, parts, swapped):
    slot = pl.program_id(0)

    @pl.when(slot == 0)
    def _():
        for tm in range(4):
            got = lax.dot_general(
                turned[tm], onehot[...], (((0,), (0,)), ((), ())), preferred_element_type=F32
            )
            for s in range(8):
                re, im = got[16 * s : 16 * s + 8], got[16 * s + 8 : 16 * s + 16]
                parts[s, 16 * tm : 16 * tm + 16] = jnp.concatenate([re, im], axis=0).astype(BF16)
                swapped[s, 16 * tm : 16 * tm + 16] = jnp.concatenate([-im, re], axis=0).astype(BF16)

    part, swap = parts[slot], swapped[slot]

    def product(i, right, j):
        return lax.dot_general(
            part[:, i * 256 : i * 256 + 256], right[:, j * 256 : j * 256 + 256],
            (((0,), (0,)), ((), ())), preferred_element_type=F32,
        )

    upper = lax.broadcasted_iota(jnp.int32, (256, 256), 0) <= lax.broadcasted_iota(jnp.int32, (256, 256), 1)
    for i in range(2):
        for j in range(2):
            if i == j:
                block = jnp.where(upper, product(i, part, j), product(i, swap, j))
            else:
                block = product(i, part if i < j else swap, j)
            out[0, i * 256 : i * 256 + 256, j * 256 : j * 256 + 256] = block * (1.0 / 32)


def correlate(turned, onehot):
    return pl.pallas_call(
        correlate_kernel,
        out_shape=jax.ShapeDtypeStruct((8, 512, 512), F32),
        grid=(8,),
        in_specs=[
            pl.BlockSpec((4, 512, 128), lambda s: (0, 0, 0)),
            pl.BlockSpec((512, 512), lambda s: (0, 0)),
        ],
        out_specs=pl.BlockSpec((1, 512, 512), lambda s: (s, 0, 0)),
        scratch_shapes=[pltpu.VMEM((8, 64, 512), BF16), pltpu.VMEM((8, 64, 512), BF16)],
        compiler_params=pltpu.CompilerParams(vmem_limit_bytes=24 << 20),
        name="correlate",
    )(turned, onehot)


def body(samples, history, station_order, channel_order, flagged):
    turned, onehot = spectra(channel_order, station_order, flagged, samples, history)
    return correlate(turned.reshape(4, 512, 128), onehot)


def solution(mesh):
    return jax.shard_map(
        body,
        mesh=mesh,
        in_specs=(P("st", "tm"), P("st", None), P(), P(), P()),
        out_specs=P(("st", "tm", "pol"), None, None),
        check_vma=False,
    )
```

```python
import functools
import math

import jax
import jax.numpy as jnp
import numpy as np
from jax import lax
from jax.experimental import pallas as pl
from jax.experimental.pallas import tpu as pltpu
from jax.sharding import PartitionSpec as P

import ml_dtypes

NFFT = 8192
FRAME_A = 32
FRAME_B = NFFT // FRAME_A
CH = 2048
TAPS = 4
LEAD = TAPS - 1
ROWS = 8
FRAMES = 8
PEERS = 256
MESH = pl.DeviceIdType.MESH
Z_OFFSETS = (1, 7, 2, 6, 3, 5, 4, 0)
BF16 = jnp.bfloat16
F32 = jnp.float32


def constants():
    bf = ml_dtypes.bfloat16
    length = TAPS * NFFT
    m = np.arange(length) + 0.5
    window = np.sinc((m - 0.5 * length) / NFFT) * (0.5 - 0.5 * np.cos(m * (2.0 * math.pi / length)))
    window = window.reshape(TAPS, NFFT).astype(np.float32)
    a = np.arange(FRAME_A)
    angle = (a[:, None] * a[None, :] % FRAME_A) * (2.0 * math.pi / FRAME_A)
    cos = np.cos(angle) / math.sqrt(FRAME_A)
    sin = -np.sin(angle) / math.sqrt(FRAME_A)
    first = np.concatenate([cos[:, :17], sin[:, 1:16]], axis=1).T.astype(bf)
    first = np.kron(first.astype(np.float32), np.eye(ROWS, dtype=np.float32)).astype(bf)
    b = np.arange(FRAME_B)
    twist = (a[:, None] * b[None, :] % NFFT) * (2.0 * math.pi / NFFT)
    twist_cos = np.repeat(np.cos(twist), ROWS, axis=0).astype(np.float32)
    twist_sin = np.repeat(np.sin(twist), ROWS, axis=0).astype(np.float32)
    f = np.arange(CH // FRAME_A)
    angle = (b[:, None] * f[None, :] % FRAME_B) * (2.0 * math.pi / FRAME_B)
    cos = (np.cos(angle) / math.sqrt(FRAME_B)).astype(bf)
    sin = (-np.sin(angle) / math.sqrt(FRAME_B)).astype(bf)
    second = np.concatenate([np.concatenate([cos, sin], 1), np.concatenate([-sin, cos], 1)], 0)
    t, p, f = np.meshgrid(np.arange(FRAMES), np.arange(2), np.arange(64), indexing="ij")
    perm = np.zeros((1024, 1024), np.float32)
    perm[(t * 128 + p * 64 + f).ravel(), (f * 16 + p * 8 + t).ravel()] = 1
    return window, first, twist_cos, twist_sin, second, perm.astype(bf)


def spectra_kernel(
    channels_h, stations_h, flags_h, samples, history, window_h, first_h, tcos_h, tsin_h, second_h, perm_h, out, onehot,
    stream, window, first, tcos, tsin, second, perm, filtered, lanes, full, messages,
    channels, stations, flags, where, place, sem, lead_sem, lead_send, send_sem, recv_sem, own_sem,
):
    st, tm, pol = lax.axis_index("st"), lax.axis_index("tm"), lax.axis_index("pol")
    z, y, w = st // 4, st % 4, tm * 2 + pol
    zs = [(z + o) % 8 for o in Z_OFFSETS]

    def each(action, o):
        yy, ww = (y + o % 4) % 4, (w + o // 4) % 8
        for j in range(8):
            action(j, zs[j] * 4 + yy, ww // 2, ww % 2)

    def when_other(j, o, action):
        if Z_OFFSETS[j]:
            action()
        else:
            pl.when(o != 0)(action)

    lead = LEAD * NFFT
    half = lead // 2
    rows = pl.ds(pl.multiple_of(pol * ROWS, ROWS), ROWS)
    moves = [
        (samples.at[rows], stream.at[:, pl.ds(lead, FRAMES * NFFT)]),
        (window_h, window), (first_h, first), (tcos_h, tcos), (tsin_h, tsin),
        (second_h, second), (perm_h, perm), (channels_h, channels), (stations_h, stations), (flags_h, flags),
    ]
    copies = [pltpu.make_async_copy(s, d, sem.at[i]) for i, (s, d) in enumerate(moves)]
    for c in copies:
        c.start()
    before = pltpu.make_async_copy(history.at[rows], stream.at[:, pl.ds(0, lead)], sem.at[len(moves)])
    pl.when(tm == 0)(before.start)

    barrier = pltpu.get_barrier_semaphore()

    def greet(o, carry):
        def signal(j, a, b, c):
            when_other(j, o, lambda: pl.semaphore_signal(
                barrier, inc=1, device_id=(a, b, c), device_id_type=MESH
            ))

        each(signal, o)
        return carry

    lax.fori_loop(0, 32, greet, 0)
    for c in copies[:2]:
        c.wait()

    def taps(lo, hi):
        def step(i, carry):
            parts = []
            for h in range(2):
                off = i // 2 * 512 + h * 256 + i % 2 * 128
                w = [
                    jnp.broadcast_to(window[k : k + 1, pl.ds(pl.multiple_of(off, 128), 128)], (ROWS, 128))
                    for k in range(TAPS)
                ]
                x = {
                    j: stream[:, pl.ds(pl.multiple_of(off + j * NFFT, 128), 128)].astype(F32)
                    for j in range(lo, hi + LEAD)
                }
                parts.append([sum(w[k] * x[t + k] for k in range(TAPS)) for t in range(lo, hi)])
            for t in range(lo, hi):
                block = jnp.concatenate([parts[0][t - lo], parts[1][t - lo]], axis=0).astype(BF16)
                filtered[
                    t, pl.ds(pl.multiple_of(i // 2 * 16, 16), 16), pl.ds(pl.multiple_of(i % 2 * 128, 128), 128)
                ] = block
            return carry

        lax.fori_loop(0, 32, step, 0)

    for c in copies[7:]:
        c.wait()
    f = channels[...] // FRAME_A
    order = lax.broadcasted_iota(jnp.int32, (16, 128), 1) % 8
    where[0:16] = f // 8 * 32 + channels[...] % FRAME_A
    where[16:32] = (8 + order - f % 8) % 8 * 16
    placing = pltpu.make_async_copy(where, place, sem.at[len(moves) + 1])
    placing.start()
    row = lax.broadcasted_iota(jnp.int32, (ROWS, 128), 0) // 2
    keep = jnp.zeros((ROWS, 128), F32)
    for i in range(ROWS // 2):
        flag = 1 - flags[stations[st * 8 + pol * 4 + i]]
        keep = jnp.where(row == i, flag.astype(F32), keep)
    keep = jnp.tile(keep, (FRAME_A, 1))

    def frame(t, carry):
        seg = jnp.dot(first[...], filtered[t], preferred_element_type=F32)
        res, ims = [], []
        for e in range(FRAME_A):
            s = min(e, FRAME_A - e)
            rs = slice(e * ROWS, (e + 1) * ROWS)
            c, n = tcos[rs, :], tsin[rs, :]
            re = seg[s * ROWS : (s + 1) * ROWS]
            if s in (0, 16):
                res.append(re * c)
                ims.append(-(re * n))
            else:
                im = seg[(16 + s) * ROWS : (17 + s) * ROWS]
                if e < 16:
                    res.append(re * c + im * n)
                    ims.append(im * c - re * n)
                else:
                    res.append(re * c - im * n)
                    ims.append(-(im * c) - re * n)
        tw = jnp.concatenate(
            [jnp.concatenate(res, axis=0).astype(BF16), jnp.concatenate(ims, axis=0).astype(BF16)], axis=1
        )
        spec = jnp.dot(tw, second[...], preferred_element_type=F32) * keep
        lanes[:, pl.ds(pl.multiple_of(t * 128, 128), 128)] = spec.astype(BF16)
        return carry

    taps(LEAD, FRAMES)
    for c in copies[2:6]:
        c.wait()
    lax.fori_loop(LEAD, FRAMES, frame, 0)

    pl.semaphore_wait(barrier, PEERS - 1)

    def lead_copy(i, b, c):
        src = samples.at[
            pl.ds(pl.multiple_of(c * ROWS, ROWS), ROWS), pl.ds(FRAMES * NFFT - lead + i * half, half)
        ]
        return pltpu.make_async_remote_copy(
            src, stream.at[:, pl.ds(i * half, half)], lead_send.at[i], lead_sem.at[i],
            device_id=(st, b, c), device_id_type=MESH,
        )

    after = (tm + 1) % 4
    across = (pol + after + 1) % 2
    leads = [lead_copy(0, after, pol), lead_copy(1, after, across)]

    @pl.when(tm != 3)
    def _():
        for c in leads:
            c.start()

    @pl.when(tm != 0)
    def _():
        for c in leads:
            c.wait_recv()

    pl.when(tm == 0)(before.wait)
    taps(0, LEAD)
    lax.fori_loop(0, LEAD, frame, 0)
    copies[6].wait()
    for q in range(4):
        turned = jnp.dot(lanes[...], perm[:, q * 256 : (q + 1) * 256], preferred_element_type=F32)
        for h in range(2):
            block = 2 * q + h
            full[block * 32 : (block + 1) * 32] = turned[:, h * 128 : (h + 1) * 128].reshape(32, ROWS, 128)

    lane = lax.broadcasted_iota(jnp.int32, (ROWS, 128), 1) // 16
    slot = tm * 64 + st * 2 + pol

    def send(o, carry):
        def gather(j, a, b, c):
            peer = a * 8 + b * 2 + c
            acc = None
            for i in range(8):
                at, col = peer // 16, peer % 16 * 8 + i
                v = pltpu.roll(full[place[at, col]], place[16 + at, col], 1)
                acc = v if acc is None else jnp.where(lane == i, v, acc)
            return acc.astype(BF16)

        def one(j, a, b, c):
            peer = a * 8 + b * 2 + c
            when_other(j, o, pltpu.make_async_remote_copy(
                messages.at[peer], out.at[slot], send_sem, recv_sem,
                device_id=(a, b, c), device_id_type=MESH,
            ).start)

        made = []
        each(lambda *at: made.append((at, gather(*at))), o)
        for (j, a, b, c), block in made:
            messages[a * 8 + b * 2 + c] = block
        each(one, o)
        return carry

    placing.wait()
    lax.fori_loop(0, 32, send, 0)
    own = pltpu.make_async_copy(messages.at[st * 8 + w], out.at[slot], own_sem)
    own.start()

    inputs = lax.broadcasted_iota(jnp.int32, (16, 512), 1)
    pair = lax.broadcasted_iota(jnp.int32, (16, 512), 0)

    def target(i, carry):
        at = jnp.zeros((16, 512), jnp.int32)
        for p in range(8):
            at = jnp.where(pair // 2 == p, 2 * stations[i * 8 + p], at)
        onehot[pl.ds(pl.multiple_of(i * 16, 16), 16), :] = (at + pair % 2 == inputs).astype(F32).astype(BF16)
        return carry

    lax.fori_loop(0, 32, target, 0)

    @pl.when(tm != 3)
    def _():
        for c in leads:
            c.wait_send()

    own.wait()
    part = pl.ds(0, PEERS - 1)
    pltpu.make_async_copy(messages.at[part], out.at[part], send_sem).wait()
    pltpu.make_async_copy(messages.at[part], out.at[part], recv_sem).wait()


def spectra(channels, stations, flags, samples, history):
    consts = [jnp.asarray(c) for c in constants()]
    hbm = pl.BlockSpec(memory_space=pltpu.HBM)
    vmem = pl.BlockSpec(memory_space=pltpu.VMEM)
    return pl.pallas_call(
        spectra_kernel,
        out_shape=[jax.ShapeDtypeStruct((PEERS, ROWS, 128), BF16), jax.ShapeDtypeStruct((512, 512), BF16)],
        in_specs=[hbm] * 11,
        out_specs=[vmem, vmem],
        scratch_shapes=[
            pltpu.VMEM((ROWS, (FRAMES + LEAD) * NFFT), BF16),
            pltpu.VMEM((TAPS, NFFT), F32),
            pltpu.VMEM((256, 256), BF16),
            pltpu.VMEM((256, 256), F32),
            pltpu.VMEM((256, 256), F32),
            pltpu.VMEM((512, 128), BF16),
            pltpu.VMEM((1024, 1024), BF16),
            pltpu.VMEM((FRAMES, 256, 256), BF16),
            pltpu.VMEM((256, 1024), BF16),
            pltpu.VMEM((256, ROWS, 128), F32),
            pltpu.VMEM((PEERS, ROWS, 128), BF16),
            pltpu.VMEM((16, 128), jnp.int32),
            pltpu.SMEM((256,), jnp.int32),
            pltpu.SMEM((256,), jnp.int32),
            pltpu.VMEM((32, 128), jnp.int32),
            pltpu.SMEM((32, 128), jnp.int32),
            pltpu.SemaphoreType.DMA((12,)),
            pltpu.SemaphoreType.DMA((2,)),
            pltpu.SemaphoreType.DMA((2,)),
        ] + [pltpu.SemaphoreType.DMA] * 3,
        compiler_params=pltpu.CompilerParams(
            vmem_limit_bytes=60 << 20, collective_id=0, has_side_effects=True
        ),
        name="spectra",
    )(channels, stations, flags, samples, history, *consts)


def correlate_kernel(turned, onehot, out, parts, swapped):
    slot = pl.program_id(0)

    @pl.when(slot == 0)
    def _():
        for tm in range(4):
            got = lax.dot_general(
                turned[tm], onehot[...], (((0,), (0,)), ((), ())), preferred_element_type=F32
            )
            for s in range(8):
                re, im = got[16 * s : 16 * s + 8], got[16 * s + 8 : 16 * s + 16]
                parts[s, 16 * tm : 16 * tm + 16] = jnp.concatenate([re, im], axis=0).astype(BF16)
                swapped[s, 16 * tm : 16 * tm + 16] = jnp.concatenate([-im, re], axis=0).astype(BF16)

    part, swap = parts[slot], swapped[slot]

    def product(i, right, j):
        return lax.dot_general(
            part[:, i * 256 : i * 256 + 256], right[:, j * 256 : j * 256 + 256],
            (((0,), (0,)), ((), ())), preferred_element_type=F32,
        )

    upper = lax.broadcasted_iota(jnp.int32, (256, 256), 0) <= lax.broadcasted_iota(jnp.int32, (256, 256), 1)
    for i in range(2):
        for j in range(2):
            if i == j:
                block = jnp.where(upper, product(i, part, j), product(i, swap, j))
            else:
                block = product(i, part if i < j else swap, j)
            out[0, i * 256 : i * 256 + 256, j * 256 : j * 256 + 256] = block * (1.0 / 32)


def correlate(turned, onehot):
    return pl.pallas_call(
        correlate_kernel,
        out_shape=jax.ShapeDtypeStruct((8, 512, 512), F32),
        grid=(8,),
        in_specs=[
            pl.BlockSpec((4, 512, 128), lambda s: (0, 0, 0)),
            pl.BlockSpec((512, 512), lambda s: (0, 0)),
        ],
        out_specs=pl.BlockSpec((1, 512, 512), lambda s: (s, 0, 0)),
        scratch_shapes=[pltpu.VMEM((8, 64, 512), BF16), pltpu.VMEM((8, 64, 512), BF16)],
        compiler_params=pltpu.CompilerParams(vmem_limit_bytes=24 << 20),
        name="correlate",
    )(turned, onehot)


def body(samples, history, station_order, channel_order, flagged):
    turned, onehot = spectra(channel_order.reshape(16, 128), station_order, flagged, samples, history)
    return correlate(turned.reshape(4, 512, 128), onehot)


def solution(mesh):
    return jax.shard_map(
        body,
        mesh=mesh,
        in_specs=(P("st", "tm"), P("st", None), P(), P(), P()),
        out_specs=P(("st", "tm", "pol"), None, None),
        check_vma=False,
    )
```

```python
import functools
import math

import jax
import jax.numpy as jnp
import numpy as np
from jax import lax
from jax.experimental import pallas as pl
from jax.experimental.pallas import tpu as pltpu
from jax.sharding import PartitionSpec as P

import ml_dtypes

NFFT = 8192
FRAME_A = 32
FRAME_B = NFFT // FRAME_A
CH = 2048
TAPS = 4
LEAD = TAPS - 1
ROWS = 8
FRAMES = 8
PEERS = 256
UNROLL = True
GROUP = 4
MESH = pl.DeviceIdType.MESH
Z_OFFSETS = (4, 3, 5, 2, 6, 1, 7, 0)
BF16 = jnp.bfloat16
F32 = jnp.float32


def constants():
    bf = ml_dtypes.bfloat16
    length = TAPS * NFFT
    m = np.arange(length) + 0.5
    window = np.sinc((m - 0.5 * length) / NFFT) * (0.5 - 0.5 * np.cos(m * (2.0 * math.pi / length)))
    window = window.reshape(TAPS, NFFT).astype(np.float32)
    a = np.arange(FRAME_A)
    angle = (a[:, None] * a[None, :] % FRAME_A) * (2.0 * math.pi / FRAME_A)
    cos = np.cos(angle) / math.sqrt(FRAME_A)
    sin = -np.sin(angle) / math.sqrt(FRAME_A)
    first = np.concatenate([cos[:, :17], sin[:, 1:16]], axis=1).T.astype(bf)
    first = np.kron(first.astype(np.float32), np.eye(ROWS, dtype=np.float32)).astype(bf)
    b = np.arange(FRAME_B)
    twist = (a[:, None] * b[None, :] % NFFT) * (2.0 * math.pi / NFFT)
    twist_cos = np.repeat(np.cos(twist), ROWS, axis=0).astype(np.float32)
    twist_sin = np.repeat(np.sin(twist), ROWS, axis=0).astype(np.float32)
    f = np.arange(CH // FRAME_A)
    angle = (b[:, None] * f[None, :] % FRAME_B) * (2.0 * math.pi / FRAME_B)
    cos = (np.cos(angle) / math.sqrt(FRAME_B)).astype(bf)
    sin = (-np.sin(angle) / math.sqrt(FRAME_B)).astype(bf)
    second = np.concatenate([np.concatenate([cos, sin, sin, cos], 1), np.concatenate([-sin, cos, cos, -sin], 1)], 0)
    t, p, f = np.meshgrid(np.arange(FRAMES), np.arange(2), np.arange(64), indexing="ij")
    perm = np.zeros((1024, 1024), np.float32)
    perm[(t * 128 + p * 64 + f).ravel(), (f * 16 + p * 8 + t).ravel()] = 1
    return window, first, twist_cos, twist_sin, second, perm.astype(bf)


def spectra_kernel(
    channels_h, stations_h, flags_h, samples, history, window_h, first_h, tcos_h, tsin_h, second_h, perm_h, out, onehot,
    stream, window, first, tcos, tsin, second, perm, filtered, lanes, chosen, messages,
    channels, stations, flags, sem, lead_sem, lead_send, send_sem, recv_sem, own_sem,
):
    st, tm, pol = lax.axis_index("st"), lax.axis_index("tm"), lax.axis_index("pol")
    z, y, w = st // 4, st % 4, tm * 2 + pol
    zs = [(z + o) % 8 for o in Z_OFFSETS]

    def each(action, o):
        yy, ww = (y + o % 4) % 4, (w + o // 4) % 8
        for j in range(8):
            action(j, zs[j] * 4 + yy, ww // 2, ww % 2)

    def when_other(j, o, action):
        if Z_OFFSETS[j]:
            action()
        else:
            pl.when(o != 0)(action)

    lead = LEAD * NFFT
    half = lead // 2
    rows = pl.ds(pl.multiple_of(pol * ROWS, ROWS), ROWS)
    moves = [
        (samples.at[rows], stream.at[:, pl.ds(lead, FRAMES * NFFT)]),
        (window_h, window), (first_h, first), (tcos_h, tcos), (tsin_h, tsin),
        (second_h, second), (perm_h, perm), (channels_h, channels), (stations_h, stations), (flags_h, flags),
    ]
    copies = [pltpu.make_async_copy(s, d, sem.at[i]) for i, (s, d) in enumerate(moves)]
    for c in copies:
        c.start()
    before = pltpu.make_async_copy(history.at[rows], stream.at[:, pl.ds(0, lead)], sem.at[len(moves)])
    pl.when(tm == 0)(before.start)

    barrier = pltpu.get_barrier_semaphore()

    def greet(o, carry):
        def signal(j, a, b, c):
            when_other(j, o, lambda: pl.semaphore_signal(
                barrier, inc=1, device_id=(a, b, c), device_id_type=MESH
            ))

        each(signal, o)
        return carry

    lax.fori_loop(0, 32, greet, 0)
    for c in copies[:2]:
        c.wait()

    def taps(lo, hi):
        def step(i, carry):
            parts = []
            for h in range(2):
                off = i // 2 * 512 + h * 256 + i % 2 * 128
                w = [
                    jnp.broadcast_to(window[k : k + 1, pl.ds(pl.multiple_of(off, 128), 128)], (ROWS, 128))
                    for k in range(TAPS)
                ]
                x = {
                    j: stream[:, pl.ds(pl.multiple_of(off + j * NFFT, 128), 128)].astype(F32)
                    for j in range(lo, hi + LEAD)
                }
                parts.append([sum(w[k] * x[t + k] for k in range(TAPS)) for t in range(lo, hi)])
            for t in range(lo, hi):
                block = jnp.concatenate([parts[0][t - lo], parts[1][t - lo]], axis=0).astype(BF16)
                filtered[
                    t, pl.ds(pl.multiple_of(i // 2 * 16, 16), 16), pl.ds(pl.multiple_of(i % 2 * 128, 128), 128)
                ] = block
            return carry

        lax.fori_loop(0, 32, step, 0)

    for c in copies[7:]:
        c.wait()
    row = lax.broadcasted_iota(jnp.int32, (ROWS, 128), 0) // 2
    keep = jnp.zeros((ROWS, 128), F32)
    for i in range(ROWS // 2):
        flag = 1 - flags[stations[st * 8 + pol * 4 + i]]
        keep = jnp.where(row == i, flag.astype(F32), keep)
    low = lax.broadcasted_iota(jnp.int32, (ROWS, 128), 1) < 64

    def frame(t, carry):
        seg = jnp.dot(first[...], filtered[t], preferred_element_type=F32)
        res, ims = [], []
        for e in range(FRAME_A):
            s = min(e, FRAME_A - e)
            rs = slice(e * ROWS, (e + 1) * ROWS)
            c, n = tcos[rs, :], tsin[rs, :]
            re = seg[s * ROWS : (s + 1) * ROWS]
            if s in (0, 16):
                res.append(re * c)
                ims.append(-(re * n))
            else:
                im = seg[(16 + s) * ROWS : (17 + s) * ROWS]
                if e < 16:
                    res.append(re * c + im * n)
                    ims.append(im * c - re * n)
                else:
                    res.append(re * c - im * n)
                    ims.append(-(im * c) - re * n)
        tw = jnp.concatenate(
            [jnp.concatenate(res, axis=0).astype(BF16), jnp.concatenate(ims, axis=0).astype(BF16)], axis=1
        )
        spec = jnp.dot(tw, second[...], preferred_element_type=F32)
        for e in range(0, FRAME_A, 2):
            one, two = (spec[i * ROWS : (i + 1) * ROWS] for i in (e, e + 1))
            both = [
                jnp.where(low, one[:, :128], two[:, 128:]) * keep,
                jnp.where(low, one[:, 128:], two[:, :128]) * keep,
            ]
            lanes[pl.ds(pl.multiple_of(t * 16, 16), 16), e * 64 : e * 64 + 128] = jnp.concatenate(both, axis=0).astype(BF16)
        return carry

    taps(LEAD, FRAMES)
    for c in copies[2:6]:
        c.wait()
    lax.fori_loop(LEAD, FRAMES, frame, 0, unroll=UNROLL)

    pl.semaphore_wait(barrier, PEERS - 1)

    def lead_copy(i, b, c):
        src = samples.at[
            pl.ds(pl.multiple_of(c * ROWS, ROWS), ROWS), pl.ds(FRAMES * NFFT - lead + i * half, half)
        ]
        return pltpu.make_async_remote_copy(
            src, stream.at[:, pl.ds(i * half, half)], lead_send.at[i], lead_sem.at[i],
            device_id=(st, b, c), device_id_type=MESH,
        )

    after = (tm + 1) % 4
    across = (pol + after + 1) % 2
    leads = [lead_copy(0, after, pol), lead_copy(1, after, across)]

    @pl.when(tm != 3)
    def _():
        for c in leads:
            c.start()

    order = channels[...]
    channels[...] = order % FRAME_A * 64 + order // FRAME_A
    at = lax.broadcasted_iota(jnp.int32, (256, 128), 0)

    def choose(i, carry):
        for h in range(2):
            wanted = jnp.broadcast_to(channels[pl.ds(2 * i + h, 1), :], (256, 128))
            for k in range(8):
                block = jnp.where(at == wanted - 256 * k, 1.0, 0.0).astype(BF16)
                chosen[i, k * 256 : (k + 1) * 256, h * 128 : (h + 1) * 128] = block
        return carry

    lax.fori_loop(0, 8, choose, 0)

    @pl.when(tm != 0)
    def _():
        for c in leads:
            c.wait_recv()

    pl.when(tm == 0)(before.wait)
    taps(0, LEAD)
    lax.fori_loop(0, LEAD, frame, 0, unroll=UNROLL)
    copies[6].wait()
    slot = tm * 64 + st * 2 + pol

    def blocks(s):
        picked = jnp.dot(lanes[...], chosen[s], preferred_element_type=F32)
        rows = []
        for h in range(2):
            first_half, second_half = [], []
            for t in range(FRAMES):
                re, im = (picked[t * 16 + p * 8 : t * 16 + p * 8 + 8, h * 128 : (h + 1) * 128] for p in range(2))
                first_half.append(jnp.where(low, re, pltpu.roll(im, 64, 1)))
                second_half.append(jnp.where(low, pltpu.roll(re, 64, 1), im))
            rows += [jnp.concatenate(first_half, axis=1), jnp.concatenate(second_half, axis=1)]
        return jnp.concatenate(rows, axis=0)

    def send(i, carry):
        near = [zs[GROUP * i + g] for g in range(GROUP)] if isinstance(i, int) else None
        stacked = jnp.concatenate([blocks(s) for s in near], axis=0).astype(BF16)
        for q in range(4):
            turned = jnp.dot(stacked, perm[:, q * 256 : (q + 1) * 256], preferred_element_type=F32).astype(BF16)
            for g, s in enumerate(near):
                for b in range(4):
                    for h in range(2):
                        messages[s * 32 + b * 8 + 2 * q + h] = turned[g * 32 + b * 8 : g * 32 + b * 8 + 8, h * 128 : (h + 1) * 128]

        def ship(o, carry):
            yy, ww = (y + o % 4) % 4, (w + o // 4) % 8
            for g, s in enumerate(near):
                a = s * 4 + yy
                when_other(GROUP * i + g, o, pltpu.make_async_remote_copy(
                    messages.at[a * 8 + ww], out.at[slot], send_sem, recv_sem,
                    device_id=(a, ww // 2, ww % 2), device_id_type=MESH,
                ).start)
            return carry

        lax.fori_loop(0, 32, ship, 0)
        return carry

    for i in range(8 // GROUP):
        send(i, 0)
    own = pltpu.make_async_copy(messages.at[st * 8 + w], out.at[slot], own_sem)
    own.start()

    inputs = lax.broadcasted_iota(jnp.int32, (16, 512), 1)
    pair = lax.broadcasted_iota(jnp.int32, (16, 512), 0)

    def target(i, carry):
        at = jnp.zeros((16, 512), jnp.int32)
        for p in range(8):
            at = jnp.where(pair // 2 == p, 2 * stations[i * 8 + p], at)
        onehot[pl.ds(pl.multiple_of(i * 16, 16), 16), :] = (at + pair % 2 == inputs).astype(F32).astype(BF16)
        return carry

    lax.fori_loop(0, 32, target, 0)

    @pl.when(tm != 3)
    def _():
        for c in leads:
            c.wait_send()

    own.wait()
    part = pl.ds(0, PEERS - 1)
    pltpu.make_async_copy(messages.at[part], out.at[part], send_sem).wait()
    pltpu.make_async_copy(messages.at[part], out.at[part], recv_sem).wait()


def spectra(channels, stations, flags, samples, history):
    consts = [jnp.asarray(c) for c in constants()]
    hbm = pl.BlockSpec(memory_space=pltpu.HBM)
    vmem = pl.BlockSpec(memory_space=pltpu.VMEM)
    return pl.pallas_call(
        spectra_kernel,
        out_shape=[jax.ShapeDtypeStruct((PEERS, ROWS, 128), BF16), jax.ShapeDtypeStruct((512, 512), BF16)],
        in_specs=[hbm] * 11,
        out_specs=[vmem, vmem],
        scratch_shapes=[
            pltpu.VMEM((ROWS, (FRAMES + LEAD) * NFFT), BF16),
            pltpu.VMEM((TAPS, NFFT), F32),
            pltpu.VMEM((256, 256), BF16),
            pltpu.VMEM((256, 256), F32),
            pltpu.VMEM((256, 256), F32),
            pltpu.VMEM((512, 256), BF16),
            pltpu.VMEM((1024, 1024), BF16),
            pltpu.VMEM((FRAMES, 256, 256), BF16),
            pltpu.VMEM((128, CH), BF16),
            pltpu.VMEM((8, CH, 256), BF16),
            pltpu.VMEM((PEERS, ROWS, 128), BF16),
            pltpu.VMEM((16, 128), jnp.int32),
            pltpu.SMEM((256,), jnp.int32),
            pltpu.SMEM((256,), jnp.int32),
            pltpu.SemaphoreType.DMA((12,)),
            pltpu.SemaphoreType.DMA((2,)),
            pltpu.SemaphoreType.DMA((2,)),
        ] + [pltpu.SemaphoreType.DMA] * 3,
        compiler_params=pltpu.CompilerParams(
            vmem_limit_bytes=60 << 20, collective_id=0, has_side_effects=True
        ),
        name="spectra",
    )(channels, stations, flags, samples, history, *consts)


def correlate_kernel(turned_h, onehot_h, out, turned, onehot, parts, swapped, blocks, in_sem, out_sem):
    loads = [pltpu.make_async_copy(onehot_h, onehot, in_sem.at[4])] + [
        pltpu.make_async_copy(turned_h.at[tm], turned.at[tm], in_sem.at[tm]) for tm in range(4)
    ]
    for c in loads:
        c.start()
    loads[0].wait()
    for tm in range(4):
        loads[tm + 1].wait()
        got = lax.dot_general(
            turned[tm], onehot[...], (((0,), (0,)), ((), ())), preferred_element_type=F32
        )
        for s in range(8):
            re, im = got[16 * s : 16 * s + 8], got[16 * s + 8 : 16 * s + 16]
            parts[s, 16 * tm : 16 * tm + 16] = jnp.concatenate([re, im], axis=0).astype(BF16)
            swapped[s, 16 * tm : 16 * tm + 16] = jnp.concatenate([-im, re], axis=0).astype(BF16)

    upper = lax.broadcasted_iota(jnp.int32, (256, 256), 0) <= lax.broadcasted_iota(jnp.int32, (256, 256), 1)

    def write(slot, i):
        rows = pl.ds(i * 256, 256)
        return pltpu.make_async_copy(blocks.at[slot, rows], out.at[slot, rows], out_sem.at[slot, i])

    def step(slot, carry):
        part, swap = parts[slot], swapped[slot]

        def product(i, right, j):
            return lax.dot_general(
                part[:, i * 256 : i * 256 + 256], right[:, j * 256 : j * 256 + 256],
                (((0,), (0,)), ((), ())), preferred_element_type=F32,
            )

        for i in range(2):
            for j in range(2):
                if i == j:
                    block = jnp.where(upper, product(i, part, j), product(i, swap, j))
                else:
                    block = product(i, part if i < j else swap, j)
                blocks[slot, i * 256 : i * 256 + 256, j * 256 : j * 256 + 256] = block * (1.0 / 32)
            write(slot, i).start()
        return carry

    lax.fori_loop(0, 8, step, 0, unroll=4)
    for slot in range(8):
        for i in range(2):
            write(slot, i).wait()


def correlate(turned, onehot):
    hbm = pl.BlockSpec(memory_space=pltpu.HBM)
    return pl.pallas_call(
        correlate_kernel,
        out_shape=jax.ShapeDtypeStruct((8, 512, 512), F32),
        in_specs=[hbm, hbm],
        out_specs=hbm,
        scratch_shapes=[
            pltpu.VMEM((4, 512, 128), BF16),
            pltpu.VMEM((512, 512), BF16),
            pltpu.VMEM((8, 64, 512), BF16),
            pltpu.VMEM((8, 64, 512), BF16),
            pltpu.VMEM((8, 512, 512), F32),
            pltpu.SemaphoreType.DMA((5,)),
            pltpu.SemaphoreType.DMA((8, 2)),
        ],
        compiler_params=pltpu.CompilerParams(vmem_limit_bytes=60 << 20),
        name="correlate",
    )(turned, onehot)


def body(samples, history, station_order, channel_order, flagged):
    turned, onehot = spectra(channel_order.reshape(16, 128), station_order, flagged, samples, history)
    return correlate(turned.reshape(4, 512, 128), onehot)


def solution(mesh):
    return jax.shard_map(
        body,
        mesh=mesh,
        in_specs=(P("st", "tm"), P("st", None), P(), P(), P()),
        out_specs=P(("st", "tm", "pol"), None, None),
        check_vma=False,
    )
```

```python
import functools
import math

import jax
import jax.numpy as jnp
import numpy as np
from jax import lax
from jax.experimental import pallas as pl
from jax.experimental.pallas import tpu as pltpu
from jax.sharding import PartitionSpec as P

import ml_dtypes

NFFT = 8192
FRAME_A = 32
FRAME_B = NFFT // FRAME_A
CH = 2048
TAPS = 4
LEAD = TAPS - 1
ROWS = 8
FRAMES = 8
PEERS = 256
UNROLL = True
GROUP = 4
MESH = pl.DeviceIdType.MESH
Z_OFFSETS = (4, 3, 5, 2, 6, 1, 7, 0)
BF16 = jnp.bfloat16
F32 = jnp.float32


def constants():
    bf = ml_dtypes.bfloat16
    length = TAPS * NFFT
    m = np.arange(length) + 0.5
    window = np.sinc((m - 0.5 * length) / NFFT) * (0.5 - 0.5 * np.cos(m * (2.0 * math.pi / length)))
    window = window.reshape(TAPS, NFFT).astype(np.float32)
    a = np.arange(FRAME_A)
    angle = (a[:, None] * a[None, :] % FRAME_A) * (2.0 * math.pi / FRAME_A)
    cos = np.cos(angle) / math.sqrt(FRAME_A)
    sin = -np.sin(angle) / math.sqrt(FRAME_A)
    first = np.concatenate([cos[:, :17], sin[:, 1:16]], axis=1).T.astype(bf)
    first = np.kron(first.astype(np.float32), np.eye(ROWS, dtype=np.float32)).astype(bf)
    b = np.arange(FRAME_B)
    twist = (a[:, None] * b[None, :] % NFFT) * (2.0 * math.pi / NFFT)
    twist_cos = np.repeat(np.cos(twist), ROWS, axis=0).astype(np.float32)
    twist_sin = np.repeat(np.sin(twist), ROWS, axis=0).astype(np.float32)
    f = np.arange(CH // FRAME_A)
    angle = (b[:, None] * f[None, :] % FRAME_B) * (2.0 * math.pi / FRAME_B)
    cos = (np.cos(angle) / math.sqrt(FRAME_B)).astype(bf)
    sin = (-np.sin(angle) / math.sqrt(FRAME_B)).astype(bf)
    second = np.concatenate([np.concatenate([cos, sin, sin, cos], 1), np.concatenate([-sin, cos, cos, -sin], 1)], 0)
    t, p, f = np.meshgrid(np.arange(FRAMES), np.arange(2), np.arange(64), indexing="ij")
    perm = np.zeros((1024, 1024), np.float32)
    perm[(t * 128 + p * 64 + f).ravel(), (f * 16 + p * 8 + t).ravel()] = 1
    return window, first, twist_cos, twist_sin, second, perm.astype(bf)


def spectra_kernel(
    channels_h, stations_h, flags_h, samples, history, window_h, first_h, tcos_h, tsin_h, second_h, perm_h, out, onehot,
    stream, window, first, tcos, tsin, second, perm, filtered, lanes, chosen, messages,
    channels, stations, flags, sem, lead_sem, lead_send, send_sem, recv_sem, own_sem,
):
    st, tm, pol = lax.axis_index("st"), lax.axis_index("tm"), lax.axis_index("pol")
    z, y, w = st // 4, st % 4, tm * 2 + pol
    zs = [(z + o) % 8 for o in Z_OFFSETS]

    def each(action, o):
        yy, ww = (y + o % 4) % 4, (w + o // 4) % 8
        for j in range(8):
            action(j, zs[j] * 4 + yy, ww // 2, ww % 2)

    def when_other(j, o, action):
        if Z_OFFSETS[j]:
            action()
        else:
            pl.when(o != 0)(action)

    lead = LEAD * NFFT
    half = lead // 2
    rows = pl.ds(pl.multiple_of(pol * ROWS, ROWS), ROWS)
    moves = [
        (samples.at[rows], stream.at[:, pl.ds(lead, FRAMES * NFFT)]),
        (window_h, window), (first_h, first), (tcos_h, tcos), (tsin_h, tsin),
        (second_h, second), (perm_h, perm), (channels_h, channels), (stations_h, stations), (flags_h, flags),
    ]
    copies = [pltpu.make_async_copy(s, d, sem.at[i]) for i, (s, d) in enumerate(moves)]
    for c in copies:
        c.start()
    before = pltpu.make_async_copy(history.at[rows], stream.at[:, pl.ds(0, lead)], sem.at[len(moves)])
    pl.when(tm == 0)(before.start)

    barrier = pltpu.get_barrier_semaphore()

    def greet(o, carry):
        def signal(j, a, b, c):
            when_other(j, o, lambda: pl.semaphore_signal(
                barrier, inc=1, device_id=(a, b, c), device_id_type=MESH
            ))

        each(signal, o)
        return carry

    lax.fori_loop(0, 32, greet, 0, unroll=4)
    for c in copies[:2]:
        c.wait()

    def taps(lo, hi):
        def step(i, carry):
            parts = []
            for h in range(2):
                off = i // 2 * 512 + h * 256 + i % 2 * 128
                w = [
                    jnp.broadcast_to(window[k : k + 1, pl.ds(pl.multiple_of(off, 128), 128)], (ROWS, 128))
                    for k in range(TAPS)
                ]
                x = {
                    j: stream[:, pl.ds(pl.multiple_of(off + j * NFFT, 128), 128)].astype(F32)
                    for j in range(lo, hi + LEAD)
                }
                parts.append([sum(w[k] * x[t + k] for k in range(TAPS)) for t in range(lo, hi)])
            for t in range(lo, hi):
                block = jnp.concatenate([parts[0][t - lo], parts[1][t - lo]], axis=0).astype(BF16)
                filtered[
                    t, pl.ds(pl.multiple_of(i // 2 * 16, 16), 16), pl.ds(pl.multiple_of(i % 2 * 128, 128), 128)
                ] = block
            return carry

        lax.fori_loop(0, 32, step, 0)

    for c in copies[7:]:
        c.wait()
    row = lax.broadcasted_iota(jnp.int32, (ROWS, 128), 0) // 2
    keep = jnp.zeros((ROWS, 128), F32)
    for i in range(ROWS // 2):
        flag = 1 - flags[stations[st * 8 + pol * 4 + i]]
        keep = jnp.where(row == i, flag.astype(F32), keep)
    low = lax.broadcasted_iota(jnp.int32, (ROWS, 128), 1) < 64

    def frame(t, carry):
        seg = jnp.dot(first[...], filtered[t], preferred_element_type=F32)
        res, ims = [], []
        for e in range(FRAME_A):
            s = min(e, FRAME_A - e)
            rs = slice(e * ROWS, (e + 1) * ROWS)
            c, n = tcos[rs, :], tsin[rs, :]
            re = seg[s * ROWS : (s + 1) * ROWS]
            if s in (0, 16):
                res.append(re * c)
                ims.append(-(re * n))
            else:
                im = seg[(16 + s) * ROWS : (17 + s) * ROWS]
                if e < 16:
                    res.append(re * c + im * n)
                    ims.append(im * c - re * n)
                else:
                    res.append(re * c - im * n)
                    ims.append(-(im * c) - re * n)
        tw = jnp.concatenate(
            [jnp.concatenate(res, axis=0).astype(BF16), jnp.concatenate(ims, axis=0).astype(BF16)], axis=1
        )
        spec = jnp.dot(tw, second[...], preferred_element_type=F32)
        for e in range(0, FRAME_A, 2):
            one, two = (spec[i * ROWS : (i + 1) * ROWS] for i in (e, e + 1))
            both = [
                jnp.where(low, one[:, :128], two[:, 128:]) * keep,
                jnp.where(low, one[:, 128:], two[:, :128]) * keep,
            ]
            lanes[pl.ds(pl.multiple_of(t * 16, 16), 16), e * 64 : e * 64 + 128] = jnp.concatenate(both, axis=0).astype(BF16)
        return carry

    taps(LEAD, FRAMES)
    for c in copies[2:6]:
        c.wait()
    lax.fori_loop(LEAD, FRAMES, frame, 0, unroll=UNROLL)

    pl.semaphore_wait(barrier, PEERS - 1)

    def lead_copy(i, b, c):
        src = samples.at[
            pl.ds(pl.multiple_of(c * ROWS, ROWS), ROWS), pl.ds(FRAMES * NFFT - lead + i * half, half)
        ]
        return pltpu.make_async_remote_copy(
            src, stream.at[:, pl.ds(i * half, half)], lead_send.at[i], lead_sem.at[i],
            device_id=(st, b, c), device_id_type=MESH,
        )

    after = (tm + 1) % 4
    across = (pol + after + 1) % 2
    leads = [lead_copy(0, after, pol), lead_copy(1, after, across)]

    @pl.when(tm != 3)
    def _():
        for c in leads:
            c.start()

    order = channels[...]
    channels[...] = order % FRAME_A * 64 + order // FRAME_A
    at = lax.broadcasted_iota(jnp.int32, (256, 128), 0)

    def choose(i, carry):
        for h in range(2):
            wanted = jnp.broadcast_to(channels[pl.ds(2 * i + h, 1), :], (256, 128))
            for k in range(8):
                block = jnp.where(at == wanted - 256 * k, 1.0, 0.0).astype(BF16)
                chosen[i, k * 256 : (k + 1) * 256, h * 128 : (h + 1) * 128] = block
        return carry

    lax.fori_loop(0, 8, choose, 0)

    @pl.when(tm != 0)
    def _():
        for c in leads:
            c.wait_recv()

    pl.when(tm == 0)(before.wait)
    taps(0, LEAD)
    lax.fori_loop(0, LEAD, frame, 0, unroll=UNROLL)
    copies[6].wait()
    slot = tm * 64 + st * 2 + pol

    def blocks(s):
        picked = jnp.dot(lanes[...], chosen[s], preferred_element_type=F32)
        rows = []
        for h in range(2):
            first_half, second_half = [], []
            for t in range(FRAMES):
                re, im = (picked[t * 16 + p * 8 : t * 16 + p * 8 + 8, h * 128 : (h + 1) * 128] for p in range(2))
                first_half.append(jnp.where(low, re, pltpu.roll(im, 64, 1)))
                second_half.append(jnp.where(low, pltpu.roll(re, 64, 1), im))
            rows += [jnp.concatenate(first_half, axis=1), jnp.concatenate(second_half, axis=1)]
        return jnp.concatenate(rows, axis=0)

    def send(i, carry):
        near = [zs[GROUP * i + g] for g in range(GROUP)] if isinstance(i, int) else None
        stacked = jnp.concatenate([blocks(s) for s in near], axis=0).astype(BF16)
        for q in range(4):
            turned = jnp.dot(stacked, perm[:, q * 256 : (q + 1) * 256], preferred_element_type=F32).astype(BF16)
            for g, s in enumerate(near):
                for b in range(4):
                    for h in range(2):
                        messages[s * 32 + b * 8 + 2 * q + h] = turned[g * 32 + b * 8 : g * 32 + b * 8 + 8, h * 128 : (h + 1) * 128]

        def ship(o, carry):
            yy, ww = (y + o % 4) % 4, (w + o // 4) % 8
            for g, s in enumerate(near):
                a = s * 4 + yy
                when_other(GROUP * i + g, o, pltpu.make_async_remote_copy(
                    messages.at[a * 8 + ww], out.at[slot], send_sem, recv_sem,
                    device_id=(a, ww // 2, ww % 2), device_id_type=MESH,
                ).start)
            return carry

        lax.fori_loop(0, 32, ship, 0, unroll=4)
        return carry

    for i in range(8 // GROUP):
        send(i, 0)
    own = pltpu.make_async_copy(messages.at[st * 8 + w], out.at[slot], own_sem)
    own.start()

    inputs = lax.broadcasted_iota(jnp.int32, (16, 512), 1)
    pair = lax.broadcasted_iota(jnp.int32, (16, 512), 0)

    def target(i, carry):
        at = jnp.zeros((16, 512), jnp.int32)
        for p in range(8):
            at = jnp.where(pair // 2 == p, 2 * stations[i * 8 + p], at)
        onehot[pl.ds(pl.multiple_of(i * 16, 16), 16), :] = (at + pair % 2 == inputs).astype(F32).astype(BF16)
        return carry

    lax.fori_loop(0, 32, target, 0)

    @pl.when(tm != 3)
    def _():
        for c in leads:
            c.wait_send()

    own.wait()
    part = pl.ds(0, PEERS - 1)
    pltpu.make_async_copy(messages.at[part], out.at[part], send_sem).wait()
    pltpu.make_async_copy(messages.at[part], out.at[part], recv_sem).wait()


def spectra(channels, stations, flags, samples, history):
    consts = [jnp.asarray(c) for c in constants()]
    hbm = pl.BlockSpec(memory_space=pltpu.HBM)
    vmem = pl.BlockSpec(memory_space=pltpu.VMEM)
    return pl.pallas_call(
        spectra_kernel,
        out_shape=[jax.ShapeDtypeStruct((PEERS, ROWS, 128), BF16), jax.ShapeDtypeStruct((512, 512), BF16)],
        in_specs=[hbm] * 11,
        out_specs=[vmem, vmem],
        scratch_shapes=[
            pltpu.VMEM((ROWS, (FRAMES + LEAD) * NFFT), BF16),
            pltpu.VMEM((TAPS, NFFT), F32),
            pltpu.VMEM((256, 256), BF16),
            pltpu.VMEM((256, 256), F32),
            pltpu.VMEM((256, 256), F32),
            pltpu.VMEM((512, 256), BF16),
            pltpu.VMEM((1024, 1024), BF16),
            pltpu.VMEM((FRAMES, 256, 256), BF16),
            pltpu.VMEM((128, CH), BF16),
            pltpu.VMEM((8, CH, 256), BF16),
            pltpu.VMEM((PEERS, ROWS, 128), BF16),
            pltpu.VMEM((16, 128), jnp.int32),
            pltpu.SMEM((256,), jnp.int32),
            pltpu.SMEM((256,), jnp.int32),
            pltpu.SemaphoreType.DMA((12,)),
            pltpu.SemaphoreType.DMA((2,)),
            pltpu.SemaphoreType.DMA((2,)),
        ] + [pltpu.SemaphoreType.DMA] * 3,
        compiler_params=pltpu.CompilerParams(
            vmem_limit_bytes=60 << 20, collective_id=0, has_side_effects=True
        ),
        name="spectra",
    )(channels, stations, flags, samples, history, *consts)


def correlate_kernel(turned_h, onehot_h, out, turned, onehot, parts, swapped, blocks, in_sem, out_sem):
    loads = [pltpu.make_async_copy(onehot_h, onehot, in_sem.at[4])] + [
        pltpu.make_async_copy(turned_h.at[tm], turned.at[:, pl.ds(tm * 128, 128)], in_sem.at[tm]) for tm in range(4)
    ]
    for c in loads:
        c.start()
    loads[0].wait()
    for c in loads[1:]:
        c.wait()
    everything = lax.dot_general(
        turned[...], onehot[...], (((0,), (0,)), ((), ())), preferred_element_type=F32
    )
    for tm in range(4):
        got = everything[tm * 128 : (tm + 1) * 128]
        for s in range(8):
            re, im = got[16 * s : 16 * s + 8], got[16 * s + 8 : 16 * s + 16]
            parts[s, 16 * tm : 16 * tm + 16] = jnp.concatenate([re, im], axis=0).astype(BF16)
            swapped[s, 16 * tm : 16 * tm + 16] = jnp.concatenate([-im, re], axis=0).astype(BF16)

    upper = lax.broadcasted_iota(jnp.int32, (256, 256), 0) <= lax.broadcasted_iota(jnp.int32, (256, 256), 1)

    def write(slot, i):
        rows = pl.ds(i * 256, 256)
        return pltpu.make_async_copy(blocks.at[slot, rows], out.at[slot, rows], out_sem.at[slot, i])

    def step(slot, carry):
        part, swap = parts[slot], swapped[slot]

        def product(i, right, j):
            return lax.dot_general(
                part[:, i * 256 : i * 256 + 256], right[:, j * 256 : j * 256 + 256],
                (((0,), (0,)), ((), ())), preferred_element_type=F32,
            )

        for i in range(2):
            for j in range(2):
                if i == j:
                    block = jnp.where(upper, product(i, part, j), product(i, swap, j))
                else:
                    block = product(i, part if i < j else swap, j)
                blocks[slot, i * 256 : i * 256 + 256, j * 256 : j * 256 + 256] = block * (1.0 / 32)
            write(slot, i).start()
        return carry

    lax.fori_loop(0, 8, step, 0, unroll=4)
    for slot in range(8):
        for i in range(2):
            write(slot, i).wait()


def correlate(turned, onehot):
    hbm = pl.BlockSpec(memory_space=pltpu.HBM)
    return pl.pallas_call(
        correlate_kernel,
        out_shape=jax.ShapeDtypeStruct((8, 512, 512), F32),
        in_specs=[hbm, hbm],
        out_specs=hbm,
        scratch_shapes=[
            pltpu.VMEM((512, 512), BF16),
            pltpu.VMEM((512, 512), BF16),
            pltpu.VMEM((8, 64, 512), BF16),
            pltpu.VMEM((8, 64, 512), BF16),
            pltpu.VMEM((8, 512, 512), F32),
            pltpu.SemaphoreType.DMA((5,)),
            pltpu.SemaphoreType.DMA((8, 2)),
        ],
        compiler_params=pltpu.CompilerParams(vmem_limit_bytes=60 << 20),
        name="correlate",
    )(turned, onehot)


def body(samples, history, station_order, channel_order, flagged):
    turned, onehot = spectra(channel_order.reshape(16, 128), station_order, flagged, samples, history)
    return correlate(turned.reshape(4, 512, 128), onehot)


def solution(mesh):
    return jax.shard_map(
        body,
        mesh=mesh,
        in_specs=(P("st", "tm"), P("st", None), P(), P(), P()),
        out_specs=P(("st", "tm", "pol"), None, None),
        check_vma=False,
    )
```
